32 devices in a mesh: rep: 4 (over y, x), shard: 8 (over z, core).
Axes of the slice: x: 2, y: 2, z: 4, core: 2. Of those that a mesh axis runs over, the one named last changes fastest.
Arguments:
- anchor_attn: float32 [2048, 2048], P('shard')
- anchor_ffn: float32 [2048, 5120], P('shard')
- local_attn: float32 [4, 2048, 2048], P('rep', 'shard'), as said below
- local_ffn: float32 [4, 2048, 5120], P('rep', 'shard'), as said below
Outputs:
- outer_attn: float32 [2048, 2048], P('shard')
- outer_ffn: float32 [2048, 5120], P('shard')
Inputs may be any that keep to these rules, and one draw needn't show every extreme that they name: `local_attn`: every replica's weights differ from the anchor. `local_ffn`: every replica's weights differ from the anchor.
All inputs are finite; a program needn't handle non-finite values.
Results may differ from the reference program's by a relative error of at most 0.0003.
Values sent between devices are 32-bit elements; how exact they have to be, the bound alone decides.
A program may use at most 64 MiB of HBM per device.

```python
import jax
import jax.numpy as jnp
from jax import lax

D = 2048
FF = 5120
REPS = 4


def make_anchor(key, columns, label):
    return jax.random.normal(jax.random.fold_in(key, label), (D, columns), jnp.float32) * D ** (-0.5)


def scale_set(key, columns, label):
    column_key = jax.random.fold_in(key, label + 20)
    row_key = jax.random.fold_in(key, label + 30)
    column_scale = jnp.exp(jax.random.uniform(column_key, (columns,), jnp.float32, 0.0, jnp.log(10.0)))
    rise = jnp.log(3.0)
    ramp = jnp.exp(rise * jnp.arange(D, dtype=jnp.float32) / D)
    row_scale = ramp * jnp.exp(jax.random.uniform(row_key, (D,), jnp.float32, 0.0, jnp.log(3.3)))
    return (row_scale, column_scale)


def replica_levels(key):
    order = jax.random.permutation(jax.random.fold_in(key, 98), REPS).astype(jnp.float32)
    jitter = jax.random.uniform(jax.random.fold_in(key, 99), (REPS,), jnp.float32, 0.2, 0.8)
    level = (order + jitter) / REPS
    return 0.25 * jnp.exp(jnp.log(16.0) * level)


def make_delta(key, columns, label):
    rows_a, cols_a = scale_set(key, D, 1)
    rows_f, cols_f = scale_set(key, FF, 2)
    expected = jnp.sum(rows_a * rows_a) * jnp.sum(cols_a * cols_a) + jnp.sum(rows_f * rows_f) * jnp.sum(cols_f * cols_f)
    normalizer = 1.0 / jnp.sqrt(expected)
    row_scale, column_scale = (rows_a, cols_a) if label == 1 else (rows_f, cols_f)
    noise_key = jax.random.fold_in(key, label + 10)
    noise = jax.random.normal(noise_key, (REPS, D, columns), jnp.float32)
    replica_scale = replica_levels(key) * normalizer
    return noise * replica_scale[:, None, None] * row_scale[None, :, None] * column_scale[None, None, :]


def draw_anchor_attn(key, part):
    return make_anchor(key, D, 1)


def draw_anchor_ffn(key, part):
    return make_anchor(key, FF, 2)


def draw_local_attn(key, part):
    return make_anchor(key, D, 1)[None] + make_delta(key, D, 1)


def draw_local_ffn(key, part):
    return make_anchor(key, FF, 2)[None] + make_delta(key, FF, 2)


def setup_inputs(seed: int = 0) -> dict:
    streams_of = jax.random.split(jax.random.key(seed), 5)
    return {
        "anchor_attn": draw_anchor_attn(jax.random.fold_in(streams_of[4], 71), 0),
        "anchor_ffn": draw_anchor_ffn(jax.random.fold_in(streams_of[4], 71), 0),
        "local_attn": draw_local_attn(jax.random.fold_in(streams_of[4], 71), 0),
        "local_ffn": draw_local_ffn(jax.random.fold_in(streams_of[4], 71), 0),
    }


def reference(anchor_attn, anchor_ffn, local_attn, local_ffn):

    def squares_of(pair):
        one_attn, one_ffn = pair
        delta_a = one_attn - anchor_attn
        delta_f = one_ffn - anchor_ffn
        return jnp.sum(delta_a * delta_a) + jnp.sum(delta_f * delta_f)
    squares = lax.map(squares_of, (local_attn, local_ffn))
    factor = jnp.minimum(jnp.float32(1.0), 1.0 / jnp.sqrt(squares))

    def accumulate(carry, item):
        total_a, total_f = carry
        one_attn, one_ffn, weight = item
        total_a = total_a + weight * (one_attn - anchor_attn)
        total_f = total_f + weight * (one_ffn - anchor_ffn)
        return ((total_a, total_f), None)
    start = (jnp.zeros_like(anchor_attn), jnp.zeros_like(anchor_ffn))
    (total_a, total_f), _ = lax.scan(accumulate, start, (local_attn, local_ffn, factor))
    return (total_a / REPS, total_f / REPS)
```

```python
import functools
import math

import jax
import jax.numpy as jnp
from jax import lax
from jax.experimental import pallas as pl
from jax.experimental.pallas import tpu as pltpu
from jax.sharding import PartitionSpec as P

MESH = pl.DeviceIdType.MESH
LANES = 128
SUB = 8


def kernel(cfg, aa, af, la, lf, oa, of, anc_a, anc_f, loc_a, loc_f,
           recv1_0, recv1_1, sum1_0, sum1_1, recv2_0, recv2_1,
           part_own, part_in, fac_own, fac_x, fac_y,
           load_sem, ps, pr, fxs, fxr, fys, fyr,
           s1s, s1r, s2s, s2r, s3s, s3r, s4s, s4r):
    nx, ny, ns, rows, width, chunks, early = cfg
    n = nx * ny
    me_r = lax.axis_index("rep")
    me_s = lax.axis_index("shard")
    x = lax.rem(me_r, nx)
    y = lax.div(me_r, nx)
    loc, anc, out = (loc_a, loc_f), (anc_a, anc_f), (oa, of)
    src = (la, lf)

    def x_peer(i):
        return {"rep": y * nx + i, "shard": me_s}

    def y_peer(i):
        return {"rep": i * nx + x, "shard": me_s}

    def s_peer(i):
        return {"rep": me_r, "shard": i}

    pieces = load_sem.shape[1]
    block = rows // pieces
    loads = []
    for k in range(pieces):
        at = pl.ds(k * block, block)
        for q, (a, b) in enumerate(((la.at[0], loc_a), (lf.at[0], loc_f), (aa, anc_a), (af, anc_f))):
            copy = pltpu.make_async_copy(a.at[at], b.at[at], load_sem.at[q, k])
            copy.start()
            loads.append(copy)

    barrier = pltpu.get_barrier_semaphore()
    for d in range(1, nx):
        pl.semaphore_signal(barrier, inc=1, device_id=x_peer(lax.rem(x + d, nx)), device_id_type=MESH)
    for d in range(1, ny):
        pl.semaphore_signal(barrier, inc=1, device_id=y_peer(lax.rem(y + d, ny)), device_id_type=MESH)
    for d in range(1, ns):
        pl.semaphore_signal(barrier, inc=1, device_id=s_peer(lax.rem(me_s + d, ns)), device_id_type=MESH)
    pl.semaphore_wait(barrier, (nx - 1) + (ny - 1) + (ns - 1))

    paths = (
        (nx, x, x_peer, ny, y, y_peer, recv1_0, sum1_0, recv2_0, fac_x),
        (ny, y, y_peer, nx, x, x_peer, recv1_1, sum1_1, recv2_1, fac_y),
    )
    piece = rows // n

    def remote(a, b, ss, rs, peer):
        return pltpu.make_async_remote_copy(
            src_ref=a, dst_ref=b, send_sem=ss, recv_sem=rs, device_id=peer, device_id_type=MESH)

    def columns(p, c):
        q, col = chunks[p][c]
        return q, pl.ds(col, width), pl.ds(c * width, width)

    count = len(chunks[0])
    stage1, stage2, stage3, stage4 = {}, {}, {}, {}

    def start1(c):
        for p in range(2):
            n1, i1, peer1, n2, i2, peer2, recv1, sum1, recv2, fac = paths[p]
            q, cols, wide = columns(p, c)
            for d in range(1, n1):
                j = lax.rem(i1 + d, n1)
                at = pl.ds(pl.multiple_of(j * (rows // n1), rows // n1), rows // n1)
                copy = remote(src[q].at[0, at, cols], recv1.at[d - 1, :, wide],
                              s1s.at[p, c, d - 1], s1r.at[p, c, d - 1], peer1(j))
                copy.start()
                stage1[p, c, d] = copy

    for c in range(early):
        start1(c)

    accs = tuple(jnp.zeros((SUB, LANES), jnp.float32) for _ in range(4))
    for k in range(pieces):
        for copy in loads[4 * k:4 * k + 4]:
            copy.wait()

        def body(g, accs):
            accs = list(accs)
            at = pl.ds(pl.multiple_of(k * block + g * SUB, SUB), SUB)
            i = 0
            for q in range(2):
                for t in range(loc[q].shape[1] // LANES):
                    lanes = pl.ds(t * LANES, LANES)
                    delta = loc[q][at, lanes] - anc[q][at, lanes]
                    accs[i % 4] = accs[i % 4] + delta * delta
                    i += 1
            return tuple(accs)

        accs = lax.fori_loop(0, block // SUB, body, accs)
    part_own[...] = (accs[0] + accs[1]) + (accs[2] + accs[3])
    sends = []
    for d in range(1, ns):
        copy = remote(part_own, part_in.at[d - 1], ps.at[d - 1], pr.at[d - 1], s_peer(lax.rem(me_s + d, ns)))
        copy.start()
        sends.append(copy)
    total = part_own[...]
    for copy in sends:
        copy.wait_recv()
    for d in range(1, ns):
        total = total + part_in[d - 1]
    squares = jnp.full((SUB, LANES), jnp.sum(total), jnp.float32)
    fac_own[...] = jnp.minimum(jnp.float32(1.0), 1.0 / jnp.sqrt(squares))
    fx, fy = [], []
    for d in range(1, nx):
        copy = remote(fac_own, fac_x.at[d - 1], fxs.at[d - 1], fxr.at[d - 1], x_peer(lax.rem(x + d, nx)))
        copy.start()
        fx.append(copy)
    for d in range(1, ny):
        copy = remote(fac_own, fac_y.at[d - 1], fys.at[d - 1], fyr.at[d - 1], y_peer(lax.rem(y + d, ny)))
        copy.start()
        fy.append(copy)
    for c in range(early, count):
        start1(c)
    for copy in fx + fy:
        copy.wait_recv()

    for c in range(count):
        for p in range(2):
            n1, i1, peer1, n2, i2, peer2, recv1, sum1, recv2, fac = paths[p]
            q, cols, wide = columns(p, c)
            for d in range(1, n1):
                stage1[p, c, d].wait_recv()
            base = i1 * (rows // n1)
            mine = fac_own[...]
            theirs = [fac[d - 1] for d in range(1, n1)]

            def body(g, carry):
                at = pl.ds(pl.multiple_of(base + g * SUB, SUB), SUB)
                to = pl.ds(pl.multiple_of(g * SUB, SUB), SUB)
                col, off = chunks[p][c][1], c * width
                for t in range(width // LANES):
                    here = pl.ds(col + t * LANES, LANES)
                    there = pl.ds(off + t * LANES, LANES)
                    anchor = anc[q][at, here]
                    value = mine * (loc[q][at, here] - anchor)
                    for d in range(1, n1):
                        value = value + theirs[d - 1] * (recv1[d - 1, to, there] - anchor)
                    sum1[to, there] = value
                return carry

            lax.fori_loop(0, rows // n1 // SUB, body, 0)
            for d in range(1, n2):
                j = lax.rem(i2 + d, n2)
                at = pl.ds(pl.multiple_of(j * piece, piece), piece)
                copy = remote(sum1.at[at, wide], recv2.at[d - 1, :, wide],
                              s2s.at[p, c, d - 1], s2r.at[p, c, d - 1], peer2(j))
                copy.start()
                stage2[p, c, d] = copy

    for c in range(count):
        for p in range(2):
            n1, i1, peer1, n2, i2, peer2, recv1, sum1, recv2, fac = paths[p]
            q, cols, wide = columns(p, c)
            for d in range(1, n2):
                stage2[p, c, d].wait_recv()
            own = i2 * piece
            place = i1 * (rows // n1) + own

            def body(g, carry):
                at = pl.ds(pl.multiple_of(own + g * SUB, SUB), SUB)
                to = pl.ds(pl.multiple_of(g * SUB, SUB), SUB)
                dst = pl.ds(pl.multiple_of(place + g * SUB, SUB), SUB)
                col, off = chunks[p][c][1], c * width
                for t in range(width // LANES):
                    there = pl.ds(off + t * LANES, LANES)
                    value = sum1[at, there]
                    for d in range(1, n2):
                        value = value + recv2[d - 1, to, there]
                    out[q][dst, pl.ds(col + t * LANES, LANES)] = value / n
                return carry

            lax.fori_loop(0, piece // SUB, body, 0)
            at = pl.ds(pl.multiple_of(place, piece), piece)
            for d in range(1, n2):
                copy = remote(out[q].at[at, cols], out[q].at[at, cols],
                              s3s.at[p, c, d - 1], s3r.at[p, c, d - 1], peer2(lax.rem(i2 + d, n2)))
                copy.start()
                stage3[p, c, d] = copy

    for c in range(count):
        for p in range(2):
            n1, i1, peer1, n2, i2, peer2, recv1, sum1, recv2, fac = paths[p]
            q, cols, wide = columns(p, c)
            for d in range(1, n2):
                stage3[p, c, d].wait_recv()
            at = pl.ds(pl.multiple_of(i1 * (rows // n1), rows // n1), rows // n1)
            for d in range(1, n1):
                copy = remote(out[q].at[at, cols], out[q].at[at, cols],
                              s4s.at[p, c, d - 1], s4r.at[p, c, d - 1], peer1(lax.rem(i1 + d, n1)))
                copy.start()
                stage4[p, c, d] = copy

    for copy in sends + fx + fy:
        copy.wait_send()
    for stage in (stage1, stage2, stage3):
        for copy in stage.values():
            copy.wait_send()
    for copy in stage4.values():
        copy.wait()


def shards(nx, ny, ns, anchor_attn, anchor_ffn, local_attn, local_ffn):
    rows, da = anchor_attn.shape
    df = anchor_ffn.shape[1]
    width = math.gcd(da // 2, df // 2)
    wide = (da + df) // 2
    chunks = tuple(
        tuple([(1, p * (df // 2) + c) for c in range(0, df // 2, width)]
              + [(0, p * (da // 2) + c) for c in range(0, da // 2, width)])
        for p in range(2))
    count = len(chunks[0])
    early = min(3, count)
    pieces = math.gcd(rows // SUB, 4)
    f32 = jnp.float32
    n = nx * ny
    vmem, dma = pltpu.VMEM, pltpu.SemaphoreType.DMA
    px, py, psh = max(nx - 1, 1), max(ny - 1, 1), max(ns - 1, 1)
    pm = max(px, py)
    scratch = [
        vmem((rows, da), f32), vmem((rows, df), f32), vmem((rows, da), f32), vmem((rows, df), f32),
        vmem((px, rows // nx, wide), f32), vmem((py, rows // ny, wide), f32),
        vmem((rows // nx, wide), f32), vmem((rows // ny, wide), f32),
        vmem((py, rows // n, wide), f32), vmem((px, rows // n, wide), f32),
        vmem((SUB, LANES), f32), vmem((psh, SUB, LANES), f32),
        vmem((SUB, LANES), f32), vmem((px, SUB, LANES), f32), vmem((py, SUB, LANES), f32),
        dma((4, pieces)), dma((psh,)), dma((psh,)),
        dma((px,)), dma((px,)), dma((py,)), dma((py,)),
    ] + [dma((2, count, pm)) for _ in range(8)]
    cfg = (nx, ny, ns, rows, width, chunks, early)
    hbm = pl.BlockSpec(memory_space=pltpu.MemorySpace.HBM)
    vm = pl.BlockSpec(memory_space=pltpu.MemorySpace.VMEM)
    return pl.pallas_call(
        functools.partial(kernel, cfg),
        out_shape=OUT(rows, da, df),
        in_specs=[hbm] * 4,
        out_specs=[vm] * 2,
        scratch_shapes=scratch,
        compiler_params=pltpu.CompilerParams(
            collective_id=0, has_side_effects=True, vmem_limit_bytes=48 * 2**20),
    )(anchor_attn, anchor_ffn, local_attn, local_ffn)


def OUT(rows, da, df):
    return [jax.ShapeDtypeStruct((rows, da), jnp.float32), jax.ShapeDtypeStruct((rows, df), jnp.float32)]


def solution(mesh):
    n = mesh.shape["rep"]
    nx = max(d for d in range(1, math.isqrt(n) + 1) if n % d == 0)
    placed = (P("shard", None), P("shard", None), P("rep", "shard", None), P("rep", "shard", None))
    return jax.shard_map(
        functools.partial(shards, nx, n // nx, mesh.shape["shard"]),
        mesh=mesh,
        in_specs=placed,
        out_specs=(P("shard", None), P("shard", None)),
        check_vma=False,
    )
```

```python
import functools
import math

import jax
import jax.numpy as jnp
from jax import lax
from jax.experimental import pallas as pl
from jax.experimental.pallas import tpu as pltpu
from jax.sharding import PartitionSpec as P

MESH = pl.DeviceIdType.MESH
LANES = 128
SUB = 8


def kernel(cfg, aa, af, la, lf, oa, of, anc_a, anc_f, loc_a, loc_f,
           recv1_0, recv1_1, sum1_0, sum1_1, recv2_0, recv2_1,
           part_own, part_in, fac_own, fac_x, fac_y,
           load_sem, ps, pr, fxs, fxr, fys, fyr,
           s1s, s1r, s2s, s2r, s3s, s3r, s4s, s4r):
    nx, ny, ns, rows, width, chunks, early = cfg
    n = nx * ny
    me_r = lax.axis_index("rep")
    me_s = lax.axis_index("shard")
    x = lax.rem(me_r, nx)
    y = lax.div(me_r, nx)
    loc, anc, out = (loc_a, loc_f), (anc_a, anc_f), (oa, of)
    src = (la, lf)

    def x_peer(i):
        return {"rep": y * nx + i, "shard": me_s}

    def y_peer(i):
        return {"rep": i * nx + x, "shard": me_s}

    def s_peer(i):
        return {"rep": me_r, "shard": i}

    pieces = load_sem.shape[1]
    block = rows // pieces
    loads = []
    for k in range(pieces):
        at = pl.ds(k * block, block)
        for q, (a, b) in enumerate(((la.at[0], loc_a), (lf.at[0], loc_f), (aa, anc_a), (af, anc_f))):
            copy = pltpu.make_async_copy(a.at[at], b.at[at], load_sem.at[q, k])
            copy.start()
            loads.append(copy)

    barrier = pltpu.get_barrier_semaphore()
    for d in range(1, nx):
        pl.semaphore_signal(barrier, inc=1, device_id=x_peer(lax.rem(x + d, nx)), device_id_type=MESH)
    for d in range(1, ny):
        pl.semaphore_signal(barrier, inc=1, device_id=y_peer(lax.rem(y + d, ny)), device_id_type=MESH)
    for d in range(1, ns):
        pl.semaphore_signal(barrier, inc=1, device_id=s_peer(lax.rem(me_s + d, ns)), device_id_type=MESH)
    pl.semaphore_wait(barrier, (nx - 1) + (ny - 1) + (ns - 1))

    paths = (
        (nx, x, x_peer, ny, y, y_peer, recv1_0, sum1_0, recv2_0, fac_x),
        (ny, y, y_peer, nx, x, x_peer, recv1_1, sum1_1, recv2_1, fac_y),
    )
    piece = rows // n

    def remote(a, b, ss, rs, peer):
        return pltpu.make_async_remote_copy(
            src_ref=a, dst_ref=b, send_sem=ss, recv_sem=rs, device_id=peer, device_id_type=MESH)

    def columns(p, c):
        q, col = chunks[p][c]
        return q, pl.ds(col, width), pl.ds(c * width, width)

    count = len(chunks[0])
    stage1, stage2, stage3, stage4 = {}, {}, {}, {}

    def start1(c):
        for p in range(2):
            n1, i1, peer1, n2, i2, peer2, recv1, sum1, recv2, fac = paths[p]
            q, cols, wide = columns(p, c)
            for d in range(1, n1):
                j = lax.rem(i1 + d, n1)
                at = pl.ds(pl.multiple_of(j * (rows // n1), rows // n1), rows // n1)
                copy = remote(src[q].at[0, at, cols], recv1.at[d - 1, :, wide],
                              s1s.at[p, c, d - 1], s1r.at[p, c, d - 1], peer1(j))
                copy.start()
                stage1[p, c, d] = copy

    for c in range(early):
        start1(c)

    accs = tuple(jnp.zeros((SUB, LANES), jnp.float32) for _ in range(4))
    for k in range(pieces):
        for copy in loads[4 * k:4 * k + 4]:
            copy.wait()

        def body(g, accs):
            accs = list(accs)
            at = pl.ds(pl.multiple_of(k * block + g * SUB, SUB), SUB)
            i = 0
            for q in range(2):
                for t in range(loc[q].shape[1] // LANES):
                    lanes = pl.ds(t * LANES, LANES)
                    delta = loc[q][at, lanes] - anc[q][at, lanes]
                    accs[i % 4] = accs[i % 4] + delta * delta
                    i += 1
            return tuple(accs)

        accs = lax.fori_loop(0, block // SUB, body, accs)
    part_own[...] = (accs[0] + accs[1]) + (accs[2] + accs[3])
    sends = []
    for d in range(1, ns):
        copy = remote(part_own, part_in.at[d - 1], ps.at[d - 1], pr.at[d - 1], s_peer(lax.rem(me_s + d, ns)))
        copy.start()
        sends.append(copy)
    total = part_own[...]
    for copy in sends:
        copy.wait_recv()
    for d in range(1, ns):
        total = total + part_in[d - 1]
    squares = jnp.full((SUB, LANES), jnp.sum(total), jnp.float32)
    fac_own[...] = jnp.minimum(jnp.float32(1.0), 1.0 / jnp.sqrt(squares))
    fx, fy = [], []
    for d in range(1, nx):
        copy = remote(fac_own, fac_x.at[d - 1], fxs.at[d - 1], fxr.at[d - 1], x_peer(lax.rem(x + d, nx)))
        copy.start()
        fx.append(copy)
    for d in range(1, ny):
        copy = remote(fac_own, fac_y.at[d - 1], fys.at[d - 1], fyr.at[d - 1], y_peer(lax.rem(y + d, ny)))
        copy.start()
        fy.append(copy)
    for c in range(early, count):
        start1(c)
    for copy in fx + fy:
        copy.wait_recv()

    for c in range(count):
        for p in range(2):
            n1, i1, peer1, n2, i2, peer2, recv1, sum1, recv2, fac = paths[p]
            q, cols, wide = columns(p, c)
            for d in range(1, n1):
                stage1[p, c, d].wait_recv()
            base = i1 * (rows // n1)
            mine = fac_own[...]
            theirs = [fac[d - 1] for d in range(1, n1)]

            def body(g, carry):
                at = pl.ds(pl.multiple_of(base + g * SUB, SUB), SUB)
                to = pl.ds(pl.multiple_of(g * SUB, SUB), SUB)
                col, off = chunks[p][c][1], c * width
                for t in range(width // LANES):
                    here = pl.ds(col + t * LANES, LANES)
                    there = pl.ds(off + t * LANES, LANES)
                    anchor = anc[q][at, here]
                    value = mine * (loc[q][at, here] - anchor)
                    for d in range(1, n1):
                        value = value + theirs[d - 1] * (recv1[d - 1, to, there] - anchor)
                    sum1[to, there] = value
                return carry

            lax.fori_loop(0, rows // n1 // SUB, body, 0)
            for d in range(1, n2):
                j = lax.rem(i2 + d, n2)
                at = pl.ds(pl.multiple_of(j * piece, piece), piece)
                copy = remote(sum1.at[at, wide], recv2.at[d - 1, :, wide],
                              s2s.at[p, c, d - 1], s2r.at[p, c, d - 1], peer2(j))
                copy.start()
                stage2[p, c, d] = copy

    for c in range(count):
        for p in range(2):
            n1, i1, peer1, n2, i2, peer2, recv1, sum1, recv2, fac = paths[p]
            q, cols, wide = columns(p, c)
            for d in range(1, n2):
                stage2[p, c, d].wait_recv()
            own = i2 * piece
            place = i1 * (rows // n1) + own

            def body(g, carry):
                at = pl.ds(pl.multiple_of(own + g * SUB, SUB), SUB)
                to = pl.ds(pl.multiple_of(g * SUB, SUB), SUB)
                dst = pl.ds(pl.multiple_of(place + g * SUB, SUB), SUB)
                col, off = chunks[p][c][1], c * width
                for t in range(width // LANES):
                    there = pl.ds(off + t * LANES, LANES)
                    value = sum1[at, there]
                    for d in range(1, n2):
                        value = value + recv2[d - 1, to, there]
                    out[q][dst, pl.ds(col + t * LANES, LANES)] = value / n
                return carry

            lax.fori_loop(0, piece // SUB, body, 0)
            at = pl.ds(pl.multiple_of(place, piece), piece)
            for d in range(1, n2):
                copy = remote(out[q].at[at, cols], out[q].at[at, cols],
                              s3s.at[p, c, d - 1], s3r.at[p, c, d - 1], peer2(lax.rem(i2 + d, n2)))
                copy.start()
                stage3[p, c, d] = copy

    for c in range(count):
        for p in range(2):
            n1, i1, peer1, n2, i2, peer2, recv1, sum1, recv2, fac = paths[p]
            q, cols, wide = columns(p, c)
            for d in range(1, n2):
                stage3[p, c, d].wait_recv()
            at = pl.ds(pl.multiple_of(i1 * (rows // n1), rows // n1), rows // n1)
            for d in range(1, n1):
                copy = remote(out[q].at[at, cols], out[q].at[at, cols],
                              s4s.at[p, c, d - 1], s4r.at[p, c, d - 1], peer1(lax.rem(i1 + d, n1)))
                copy.start()
                stage4[p, c, d] = copy

    for copy in sends + fx + fy:
        copy.wait_send()
    for stage in (stage1, stage2, stage3):
        for copy in stage.values():
            copy.wait_send()
    for copy in stage4.values():
        copy.wait()


def shards(nx, ny, ns, anchor_attn, anchor_ffn, local_attn, local_ffn):
    rows, da = anchor_attn.shape
    df = anchor_ffn.shape[1]
    width = math.gcd(da // 2, df // 2)
    wide = (da + df) // 2
    chunks = tuple(
        tuple([(1, p * (df // 2) + c) for c in range(0, df // 2, width)]
              + [(0, p * (da // 2) + c) for c in range(0, da // 2, width)])
        for p in range(2))
    count = len(chunks[0])
    early = min(3, count)
    pieces = math.gcd(rows // SUB, 4)
    f32 = jnp.float32
    n = nx * ny
    vmem, dma = pltpu.VMEM, pltpu.SemaphoreType.DMA
    px, py, psh = max(nx - 1, 1), max(ny - 1, 1), max(ns - 1, 1)
    pm = max(px, py)
    scratch = [
        vmem((rows, da), f32), vmem((rows, df), f32), vmem((rows, da), f32), vmem((rows, df), f32),
        vmem((px, rows // nx, wide), f32), vmem((py, rows // ny, wide), f32),
        vmem((rows // nx, wide), f32), vmem((rows // ny, wide), f32),
        vmem((py, rows // n, wide), f32), vmem((px, rows // n, wide), f32),
        vmem((SUB, LANES), f32), vmem((psh, SUB, LANES), f32),
        vmem((SUB, LANES), f32), vmem((px, SUB, LANES), f32), vmem((py, SUB, LANES), f32),
        dma((4, pieces)), dma((psh,)), dma((psh,)),
        dma((px,)), dma((px,)), dma((py,)), dma((py,)),
    ] + [dma((2, count, pm)) for _ in range(8)]
    cfg = (nx, ny, ns, rows, width, chunks, early)
    hbm = pl.BlockSpec(memory_space=pltpu.MemorySpace.HBM)
    vm = pl.BlockSpec(memory_space=pltpu.MemorySpace.VMEM)
    return pl.pallas_call(
        functools.partial(kernel, cfg),
        out_shape=OUT(rows, da, df),
        in_specs=[hbm] * 4,
        out_specs=[vm] * 2,
        scratch_shapes=scratch,
        compiler_params=pltpu.CompilerParams(
            collective_id=0, has_side_effects=True, vmem_limit_bytes=52 * 2**20),
    )(anchor_attn, anchor_ffn, local_attn, local_ffn)


def OUT(rows, da, df):
    return [pltpu.VMEM((rows, da), jnp.float32), pltpu.VMEM((rows, df), jnp.float32)]


def solution(mesh):
    n = mesh.shape["rep"]
    nx = max(d for d in range(1, math.isqrt(n) + 1) if n % d == 0)
    placed = (P("shard", None), P("shard", None), P("rep", "shard", None), P("rep", "shard", None))
    return jax.shard_map(
        functools.partial(shards, nx, n // nx, mesh.shape["shard"]),
        mesh=mesh,
        in_specs=placed,
        out_specs=(P("shard", None), P("shard", None)),
        check_vma=False,
    )
```

```python
import functools
import math

import jax
import jax.numpy as jnp
from jax import lax
from jax.experimental import pallas as pl
from jax.experimental.pallas import tpu as pltpu
from jax.sharding import PartitionSpec as P

MESH = pl.DeviceIdType.MESH
LANES = 128
SUB = 8


def kernel(cfg, aa, af, la, lf, oa, of, anc_a, anc_f, loc_a, loc_f,
           recv1_0, recv1_1, sum1_0, sum1_1, recv2_0, recv2_1,
           part_own, part_up, part_down, part_in, fac_own, fac_x, fac_y,
           load_sem, ps, pr, fxs, fxr, fys, fyr,
           s1s, s1r, s2s, s2r, s3s, s3r, s4s, s4r):
    nx, ny, ns, rows, width, chunks, early = cfg
    n = nx * ny
    me_r = lax.axis_index("rep")
    me_s = lax.axis_index("shard")
    x = lax.rem(me_r, nx)
    y = lax.div(me_r, nx)
    loc, anc, out = (loc_a, loc_f), (anc_a, anc_f), (oa, of)
    src = (la, lf)

    def x_peer(i):
        return {"rep": y * nx + i, "shard": me_s}

    def y_peer(i):
        return {"rep": i * nx + x, "shard": me_s}

    def s_peer(i):
        return {"rep": me_r, "shard": i}

    pieces = load_sem.shape[1]
    block = rows // pieces
    loads = []
    for k in range(pieces):
        at = pl.ds(k * block, block)
        for q, (a, b) in enumerate(((la.at[0], loc_a), (lf.at[0], loc_f), (aa, anc_a), (af, anc_f))):
            copy = pltpu.make_async_copy(a.at[at], b.at[at], load_sem.at[q, k])
            copy.start()
            loads.append(copy)

    part_in[...] = jnp.zeros_like(part_in)

    has_next, has_prev = me_s < ns - 1, me_s > 0
    barrier = pltpu.get_barrier_semaphore()

    @pl.when(has_next)
    def _():
        pl.semaphore_signal(barrier, inc=1, device_id=s_peer(me_s + 1), device_id_type=MESH)

    @pl.when(has_prev)
    def _():
        pl.semaphore_signal(barrier, inc=1, device_id=s_peer(me_s - 1), device_id_type=MESH)

    for d in range(1, nx):
        pl.semaphore_signal(barrier, inc=1, device_id=x_peer(lax.rem(x + d, nx)), device_id_type=MESH)
    for d in range(1, ny):
        pl.semaphore_signal(barrier, inc=1, device_id=y_peer(lax.rem(y + d, ny)), device_id_type=MESH)
    near = jnp.where(has_next, 1, 0) + jnp.where(has_prev, 1, 0)
    pl.semaphore_wait(barrier, (nx - 1) + (ny - 1) + near)

    paths = (
        (nx, x, x_peer, ny, y, y_peer, recv1_0, sum1_0, recv2_0, fac_x),
        (ny, y, y_peer, nx, x, x_peer, recv1_1, sum1_1, recv2_1, fac_y),
    )
    piece = rows // n

    def remote(a, b, ss, rs, peer):
        return pltpu.make_async_remote_copy(
            src_ref=a, dst_ref=b, send_sem=ss, recv_sem=rs, device_id=peer, device_id_type=MESH)

    def columns(p, c):
        q, col = chunks[p][c]
        return q, pl.ds(col, width), pl.ds(c * width, width)

    count = len(chunks[0])
    stage1, stage2, stage3, stage4 = {}, {}, {}, {}

    def start1(c):
        for p in range(2):
            n1, i1, peer1, n2, i2, peer2, recv1, sum1, recv2, fac = paths[p]
            q, cols, wide = columns(p, c)
            for d in range(1, n1):
                j = lax.rem(i1 + d, n1)
                at = pl.ds(pl.multiple_of(j * (rows // n1), rows // n1), rows // n1)
                copy = remote(src[q].at[0, at, cols], recv1.at[d - 1, :, wide],
                              s1s.at[p, c, d - 1], s1r.at[p, c, d - 1], peer1(j))
                copy.start()
                stage1[p, c, d] = copy

    for c in range(early):
        start1(c)

    accs = tuple(jnp.zeros((SUB, LANES), jnp.float32) for _ in range(4))
    for k in range(pieces):
        for copy in loads[4 * k:4 * k + 4]:
            copy.wait()

        def body(g, accs):
            accs = list(accs)
            at = pl.ds(pl.multiple_of(k * block + g * SUB, SUB), SUB)
            i = 0
            for q in range(2):
                for t in range(loc[q].shape[1] // LANES):
                    lanes = pl.ds(t * LANES, LANES)
                    delta = loc[q][at, lanes] - anc[q][at, lanes]
                    accs[i % 4] = accs[i % 4] + delta * delta
                    i += 1
            return tuple(accs)

        accs = lax.fori_loop(0, block // SUB, body, accs)
    part_own[...] = (accs[0] + accs[1]) + (accs[2] + accs[3])
    up = remote(part_up, part_in.at[0], ps.at[0], pr.at[0], s_peer(lax.rem(me_s + 1, ns)))
    down = remote(part_down, part_in.at[1], ps.at[1], pr.at[1], s_peer(lax.rem(me_s + ns - 1, ns)))

    def pass_up():
        @pl.when(has_prev)
        def _():
            up.wait_recv()

        part_up[...] = part_own[...] + part_in[0]

        @pl.when(has_next)
        def _():
            up.start()

    def pass_down():
        @pl.when(has_next)
        def _():
            down.wait_recv()

        part_down[...] = part_own[...] + part_in[1]

        @pl.when(has_prev)
        def _():
            down.start()

    @pl.when(me_s < ns // 2)
    def _():
        pass_up()
        pass_down()

    @pl.when(me_s >= ns // 2)
    def _():
        pass_down()
        pass_up()

    total = part_own[...] + (part_in[0] + part_in[1])
    squares = jnp.full((SUB, LANES), jnp.sum(total), jnp.float32)
    fac_own[...] = jnp.minimum(jnp.float32(1.0), 1.0 / jnp.sqrt(squares))
    fx, fy = [], []
    for d in range(1, nx):
        copy = remote(fac_own, fac_x.at[d - 1], fxs.at[d - 1], fxr.at[d - 1], x_peer(lax.rem(x + d, nx)))
        copy.start()
        fx.append(copy)
    for d in range(1, ny):
        copy = remote(fac_own, fac_y.at[d - 1], fys.at[d - 1], fyr.at[d - 1], y_peer(lax.rem(y + d, ny)))
        copy.start()
        fy.append(copy)
    for c in range(early, count):
        start1(c)
    for copy in fx + fy:
        copy.wait_recv()

    for c in range(count):
        for p in range(2):
            n1, i1, peer1, n2, i2, peer2, recv1, sum1, recv2, fac = paths[p]
            q, cols, wide = columns(p, c)
            for d in range(1, n1):
                stage1[p, c, d].wait_recv()
            base = i1 * (rows // n1)
            mine = fac_own[...]
            theirs = [fac[d - 1] for d in range(1, n1)]

            def body(g, carry):
                at = pl.ds(pl.multiple_of(base + g * SUB, SUB), SUB)
                to = pl.ds(pl.multiple_of(g * SUB, SUB), SUB)
                col, off = chunks[p][c][1], c * width
                for t in range(width // LANES):
                    here = pl.ds(col + t * LANES, LANES)
                    there = pl.ds(off + t * LANES, LANES)
                    anchor = anc[q][at, here]
                    value = mine * (loc[q][at, here] - anchor)
                    for d in range(1, n1):
                        value = value + theirs[d - 1] * (recv1[d - 1, to, there] - anchor)
                    sum1[to, there] = value
                return carry

            lax.fori_loop(0, rows // n1 // SUB, body, 0)
            for d in range(1, n2):
                j = lax.rem(i2 + d, n2)
                at = pl.ds(pl.multiple_of(j * piece, piece), piece)
                copy = remote(sum1.at[at, wide], recv2.at[d - 1, :, wide],
                              s2s.at[p, c, d - 1], s2r.at[p, c, d - 1], peer2(j))
                copy.start()
                stage2[p, c, d] = copy

    for c in range(count):
        for p in range(2):
            n1, i1, peer1, n2, i2, peer2, recv1, sum1, recv2, fac = paths[p]
            q, cols, wide = columns(p, c)
            for d in range(1, n2):
                stage2[p, c, d].wait_recv()
            own = i2 * piece
            place = i1 * (rows // n1) + own

            def body(g, carry):
                at = pl.ds(pl.multiple_of(own + g * SUB, SUB), SUB)
                to = pl.ds(pl.multiple_of(g * SUB, SUB), SUB)
                dst = pl.ds(pl.multiple_of(place + g * SUB, SUB), SUB)
                col, off = chunks[p][c][1], c * width
                for t in range(width // LANES):
                    there = pl.ds(off + t * LANES, LANES)
                    value = sum1[at, there]
                    for d in range(1, n2):
                        value = value + recv2[d - 1, to, there]
                    out[q][dst, pl.ds(col + t * LANES, LANES)] = value / n
                return carry

            lax.fori_loop(0, piece // SUB, body, 0)
            at = pl.ds(pl.multiple_of(place, piece), piece)
            for d in range(1, n2):
                copy = remote(out[q].at[at, cols], out[q].at[at, cols],
                              s3s.at[p, c, d - 1], s3r.at[p, c, d - 1], peer2(lax.rem(i2 + d, n2)))
                copy.start()
                stage3[p, c, d] = copy

    for c in range(count):
        for p in range(2):
            n1, i1, peer1, n2, i2, peer2, recv1, sum1, recv2, fac = paths[p]
            q, cols, wide = columns(p, c)
            for d in range(1, n2):
                stage3[p, c, d].wait_recv()
            at = pl.ds(pl.multiple_of(i1 * (rows // n1), rows // n1), rows // n1)
            for d in range(1, n1):
                copy = remote(out[q].at[at, cols], out[q].at[at, cols],
                              s4s.at[p, c, d - 1], s4r.at[p, c, d - 1], peer1(lax.rem(i1 + d, n1)))
                copy.start()
                stage4[p, c, d] = copy

    @pl.when(has_next)
    def _():
        up.wait_send()

    @pl.when(has_prev)
    def _():
        down.wait_send()

    for copy in fx + fy:
        copy.wait_send()
    for stage in (stage1, stage2, stage3):
        for copy in stage.values():
            copy.wait_send()
    for copy in stage4.values():
        copy.wait()


def shards(nx, ny, ns, anchor_attn, anchor_ffn, local_attn, local_ffn):
    rows, da = anchor_attn.shape
    df = anchor_ffn.shape[1]
    width = math.gcd(da // 2, df // 2)
    wide = (da + df) // 2
    chunks = tuple(
        tuple([(1, p * (df // 2) + c) for c in range(0, df // 2, width)]
              + [(0, p * (da // 2) + c) for c in range(0, da // 2, width)])
        for p in range(2))
    count = len(chunks[0])
    early = min(4, count)
    pieces = math.gcd(rows // SUB, 4)
    f32 = jnp.float32
    n = nx * ny
    vmem, dma = pltpu.VMEM, pltpu.SemaphoreType.DMA
    px, py = max(nx - 1, 1), max(ny - 1, 1)
    pm = max(px, py)
    scratch = [
        vmem((rows, da), f32), vmem((rows, df), f32), vmem((rows, da), f32), vmem((rows, df), f32),
        vmem((px, rows // nx, wide), f32), vmem((py, rows // ny, wide), f32),
        vmem((rows // nx, wide), f32), vmem((rows // ny, wide), f32),
        vmem((py, rows // n, wide), f32), vmem((px, rows // n, wide), f32),
        vmem((SUB, LANES), f32), vmem((SUB, LANES), f32), vmem((SUB, LANES), f32), vmem((2, SUB, LANES), f32),
        vmem((SUB, LANES), f32), vmem((px, SUB, LANES), f32), vmem((py, SUB, LANES), f32),
        dma((4, pieces)), dma((2,)), dma((2,)),
        dma((px,)), dma((px,)), dma((py,)), dma((py,)),
    ] + [dma((2, count, pm)) for _ in range(8)]
    cfg = (nx, ny, ns, rows, width, chunks, early)
    hbm = pl.BlockSpec(memory_space=pltpu.MemorySpace.HBM)
    vm = pl.BlockSpec(memory_space=pltpu.MemorySpace.VMEM)
    out = pl.pallas_call(
        functools.partial(kernel, cfg),
        out_shape=OUT(rows, da, df),
        in_specs=[hbm] * 4,
        out_specs=[vm] * 2,
        scratch_shapes=scratch,
        compiler_params=pltpu.CompilerParams(
            collective_id=0, has_side_effects=True, vmem_limit_bytes=52 * 2**20),
    )(anchor_attn, anchor_ffn, local_attn, local_ffn)
    return write_out(*out)


def write_kernel(a, b, oa, ob, sem):
    pieces = sem.shape[1]
    block = a.shape[0] // pieces
    copies = []
    for k in range(pieces):
        at = pl.ds(k * block, block)
        for q, (src, dst) in enumerate(((b, ob), (a, oa))):
            copy = pltpu.make_async_copy(src.at[at], dst.at[at], sem.at[q, k])
            copy.start()
            copies.append(copy)
    for copy in copies:
        copy.wait()


def write_out(a, b):
    pieces = math.gcd(a.shape[0] // SUB, 4)
    return pl.pallas_call(
        write_kernel,
        out_shape=[jax.ShapeDtypeStruct(v.shape, v.dtype) for v in (a, b)],
        in_specs=[pl.BlockSpec(memory_space=pltpu.MemorySpace.VMEM)] * 2,
        out_specs=[pl.BlockSpec(memory_space=pltpu.MemorySpace.HBM)] * 2,
        scratch_shapes=[pltpu.SemaphoreType.DMA((2, pieces))],
        compiler_params=pltpu.CompilerParams(vmem_limit_bytes=16 * 2**20),
    )(a, b)


def OUT(rows, da, df):
    return [pltpu.VMEM((rows, da), jnp.float32), pltpu.VMEM((rows, df), jnp.float32)]


def solution(mesh):
    n = mesh.shape["rep"]
    nx = max(d for d in range(1, math.isqrt(n) + 1) if n % d == 0)
    placed = (P("shard", None), P("shard", None), P("rep", "shard", None), P("rep", "shard", None))
    return jax.shard_map(
        functools.partial(shards, nx, n // nx, mesh.shape["shard"]),
        mesh=mesh,
        in_specs=placed,
        out_specs=(P("shard", None), P("shard", None)),
        check_vma=False,
    )
```

```python
import functools
import math

import jax
import jax.numpy as jnp
from jax import lax
from jax.experimental import pallas as pl
from jax.experimental.pallas import tpu as pltpu
from jax.sharding import PartitionSpec as P

MESH = pl.DeviceIdType.MESH
LANES = 128
SUB = 8


def kernel(cfg, aa, af, la, lf, oa, of, anc_a, anc_f, loc_a, loc_f,
           recv1_0, recv1_1, sum1_0, sum1_1, recv2_0, recv2_1,
           part_own, part_up, part_down, part_in, fac_own, fac_x, fac_y,
           load_sem, ps, pr, fxs, fxr, fys, fyr,
           s1s, s1r, s2s, s2r, s3s, s3r, s4s, s4r):
    nx, ny, ns, rows, width, chunks, early = cfg
    n = nx * ny
    me_r = lax.axis_index("rep")
    me_s = lax.axis_index("shard")
    x = lax.rem(me_r, nx)
    y = lax.div(me_r, nx)
    loc, anc, out = (loc_a, loc_f), (anc_a, anc_f), (oa, of)
    src = (la, lf)

    def x_peer(i):
        return {"rep": y * nx + i, "shard": me_s}

    def y_peer(i):
        return {"rep": i * nx + x, "shard": me_s}

    def s_peer(i):
        return {"rep": me_r, "shard": i}

    part_in[...] = jnp.zeros_like(part_in)

    has_next, has_prev = me_s < ns - 1, me_s > 0
    barrier = pltpu.get_barrier_semaphore()

    @pl.when(has_next)
    def _():
        pl.semaphore_signal(barrier, inc=1, device_id=s_peer(me_s + 1), device_id_type=MESH)

    @pl.when(has_prev)
    def _():
        pl.semaphore_signal(barrier, inc=1, device_id=s_peer(me_s - 1), device_id_type=MESH)

    for d in range(1, nx):
        pl.semaphore_signal(barrier, inc=1, device_id=x_peer(lax.rem(x + d, nx)), device_id_type=MESH)
    for d in range(1, ny):
        pl.semaphore_signal(barrier, inc=1, device_id=y_peer(lax.rem(y + d, ny)), device_id_type=MESH)
    near = jnp.where(has_next, 1, 0) + jnp.where(has_prev, 1, 0)
    pl.semaphore_wait(barrier, (nx - 1) + (ny - 1) + near)

    paths = (
        (nx, x, x_peer, ny, y, y_peer, recv1_0, sum1_0, recv2_0, fac_x),
        (ny, y, y_peer, nx, x, x_peer, recv1_1, sum1_1, recv2_1, fac_y),
    )
    piece = rows // n

    def remote(a, b, ss, rs, peer):
        return pltpu.make_async_remote_copy(
            src_ref=a, dst_ref=b, send_sem=ss, recv_sem=rs, device_id=peer, device_id_type=MESH)

    def columns(p, c):
        q, col = chunks[p][c]
        return q, pl.ds(col, width), pl.ds(c * width, width)

    count = len(chunks[0])
    stage1, stage2, stage3, stage4 = {}, {}, {}, {}

    def start1(c):
        for p in range(2):
            n1, i1, peer1, n2, i2, peer2, recv1, sum1, recv2, fac = paths[p]
            q, cols, wide = columns(p, c)
            for d in range(1, n1):
                j = lax.rem(i1 + d, n1)
                at = pl.ds(pl.multiple_of(j * (rows // n1), rows // n1), rows // n1)
                copy = remote(src[q].at[0, at, cols], recv1.at[d - 1, :, wide],
                              s1s.at[p, c, d - 1], s1r.at[p, c, d - 1], peer1(j))
                copy.start()
                stage1[p, c, d] = copy

    start1(0)

    pieces = load_sem.shape[1]
    block = rows // pieces
    loads = []
    for k in range(pieces):
        at = pl.ds(k * block, block)
        for q, (a, b) in enumerate(((la.at[0], loc_a), (lf.at[0], loc_f), (aa, anc_a), (af, anc_f))):
            copy = pltpu.make_async_copy(a.at[at], b.at[at], load_sem.at[q, k])
            copy.start()
            loads.append(copy)

    for c in range(1, early):
        start1(c)

    accs = tuple(jnp.zeros((SUB, LANES), jnp.float32) for _ in range(4))
    for k in range(pieces):
        for copy in loads[4 * k:4 * k + 4]:
            copy.wait()

        def body(g, accs):
            accs = list(accs)
            at = pl.ds(pl.multiple_of(k * block + g * SUB, SUB), SUB)
            i = 0
            for q in range(2):
                for t in range(loc[q].shape[1] // LANES):
                    lanes = pl.ds(t * LANES, LANES)
                    delta = loc[q][at, lanes] - anc[q][at, lanes]
                    accs[i % 4] = accs[i % 4] + delta * delta
                    i += 1
            return tuple(accs)

        accs = lax.fori_loop(0, block // SUB, body, accs)
    part_own[...] = (accs[0] + accs[1]) + (accs[2] + accs[3])
    up = remote(part_up, part_in.at[0], ps.at[0], pr.at[0], s_peer(lax.rem(me_s + 1, ns)))
    down = remote(part_down, part_in.at[1], ps.at[1], pr.at[1], s_peer(lax.rem(me_s + ns - 1, ns)))

    def pass_up():
        @pl.when(has_prev)
        def _():
            up.wait_recv()

        part_up[...] = part_own[...] + part_in[0]

        @pl.when(has_next)
        def _():
            up.start()

    def pass_down():
        @pl.when(has_next)
        def _():
            down.wait_recv()

        part_down[...] = part_own[...] + part_in[1]

        @pl.when(has_prev)
        def _():
            down.start()

    @pl.when(me_s < ns // 2)
    def _():
        pass_up()
        pass_down()

    @pl.when(me_s >= ns // 2)
    def _():
        pass_down()
        pass_up()

    total = part_own[...] + (part_in[0] + part_in[1])
    squares = jnp.full((SUB, LANES), jnp.sum(total), jnp.float32)
    fac_own[...] = jnp.minimum(jnp.float32(1.0), 1.0 / jnp.sqrt(squares))
    fx, fy = [], []
    for d in range(1, nx):
        copy = remote(fac_own, fac_x.at[d - 1], fxs.at[d - 1], fxr.at[d - 1], x_peer(lax.rem(x + d, nx)))
        copy.start()
        fx.append(copy)
    for d in range(1, ny):
        copy = remote(fac_own, fac_y.at[d - 1], fys.at[d - 1], fyr.at[d - 1], y_peer(lax.rem(y + d, ny)))
        copy.start()
        fy.append(copy)
    for c in range(early, count):
        start1(c)
    for copy in fx + fy:
        copy.wait_recv()

    for c in range(count):
        for p in range(2):
            n1, i1, peer1, n2, i2, peer2, recv1, sum1, recv2, fac = paths[p]
            q, cols, wide = columns(p, c)
            for d in range(1, n1):
                stage1[p, c, d].wait_recv()
            base = i1 * (rows // n1)
            mine = fac_own[...]
            theirs = [fac[d - 1] for d in range(1, n1)]

            def body(g, carry):
                at = pl.ds(pl.multiple_of(base + g * SUB, SUB), SUB)
                to = pl.ds(pl.multiple_of(g * SUB, SUB), SUB)
                col, off = chunks[p][c][1], c * width
                for t in range(width // LANES):
                    here = pl.ds(col + t * LANES, LANES)
                    there = pl.ds(off + t * LANES, LANES)
                    anchor = anc[q][at, here]
                    value = mine * (loc[q][at, here] - anchor)
                    for d in range(1, n1):
                        value = value + theirs[d - 1] * (recv1[d - 1, to, there] - anchor)
                    sum1[to, there] = value
                return carry

            lax.fori_loop(0, rows // n1 // SUB, body, 0)
            for d in range(1, n2):
                j = lax.rem(i2 + d, n2)
                at = pl.ds(pl.multiple_of(j * piece, piece), piece)
                copy = remote(sum1.at[at, wide], recv2.at[d - 1, :, wide],
                              s2s.at[p, c, d - 1], s2r.at[p, c, d - 1], peer2(j))
                copy.start()
                stage2[p, c, d] = copy

    for c in range(count):
        for p in range(2):
            n1, i1, peer1, n2, i2, peer2, recv1, sum1, recv2, fac = paths[p]
            q, cols, wide = columns(p, c)
            for d in range(1, n2):
                stage2[p, c, d].wait_recv()
            own = i2 * piece
            place = i1 * (rows // n1) + own

            def body(g, carry):
                at = pl.ds(pl.multiple_of(own + g * SUB, SUB), SUB)
                to = pl.ds(pl.multiple_of(g * SUB, SUB), SUB)
                dst = pl.ds(pl.multiple_of(place + g * SUB, SUB), SUB)
                col, off = chunks[p][c][1], c * width
                for t in range(width // LANES):
                    there = pl.ds(off + t * LANES, LANES)
                    value = sum1[at, there]
                    for d in range(1, n2):
                        value = value + recv2[d - 1, to, there]
                    out[q][dst, pl.ds(col + t * LANES, LANES)] = value / n
                return carry

            lax.fori_loop(0, piece // SUB, body, 0)
            at = pl.ds(pl.multiple_of(place, piece), piece)
            for d in range(1, n2):
                copy = remote(out[q].at[at, cols], out[q].at[at, cols],
                              s3s.at[p, c, d - 1], s3r.at[p, c, d - 1], peer2(lax.rem(i2 + d, n2)))
                copy.start()
                stage3[p, c, d] = copy

    for c in range(count):
        for p in range(2):
            n1, i1, peer1, n2, i2, peer2, recv1, sum1, recv2, fac = paths[p]
            q, cols, wide = columns(p, c)
            for d in range(1, n2):
                stage3[p, c, d].wait_recv()
            at = pl.ds(pl.multiple_of(i1 * (rows // n1), rows // n1), rows // n1)
            for d in range(1, n1):
                copy = remote(out[q].at[at, cols], out[q].at[at, cols],
                              s4s.at[p, c, d - 1], s4r.at[p, c, d - 1], peer1(lax.rem(i1 + d, n1)))
                copy.start()
                stage4[p, c, d] = copy

    @pl.when(has_next)
    def _():
        up.wait_send()

    @pl.when(has_prev)
    def _():
        down.wait_send()

    for copy in fx + fy:
        copy.wait_send()
    for stage in (stage1, stage2, stage3):
        for copy in stage.values():
            copy.wait_send()
    for copy in stage4.values():
        copy.wait()


def shards(nx, ny, ns, anchor_attn, anchor_ffn, local_attn, local_ffn):
    rows, da = anchor_attn.shape
    df = anchor_ffn.shape[1]
    width = math.gcd(da // 2, df // 2)
    wide = (da + df) // 2
    chunks = tuple(
        tuple([(1, p * (df // 2) + c) for c in range(0, df // 2, width)]
              + [(0, p * (da // 2) + c) for c in range(0, da // 2, width)])
        for p in range(2))
    count = len(chunks[0])
    early = min(4, count)
    pieces = math.gcd(rows // SUB, 4)
    f32 = jnp.float32
    n = nx * ny
    vmem, dma = pltpu.VMEM, pltpu.SemaphoreType.DMA
    px, py = max(nx - 1, 1), max(ny - 1, 1)
    pm = max(px, py)
    scratch = [
        vmem((rows, da), f32), vmem((rows, df), f32), vmem((rows, da), f32), vmem((rows, df), f32),
        vmem((px, rows // nx, wide), f32), vmem((py, rows // ny, wide), f32),
        vmem((rows // nx, wide), f32), vmem((rows // ny, wide), f32),
        vmem((py, rows // n, wide), f32), vmem((px, rows // n, wide), f32),
        vmem((SUB, LANES), f32), vmem((SUB, LANES), f32), vmem((SUB, LANES), f32), vmem((2, SUB, LANES), f32),
        vmem((SUB, LANES), f32), vmem((px, SUB, LANES), f32), vmem((py, SUB, LANES), f32),
        dma((4, pieces)), dma((2,)), dma((2,)),
        dma((px,)), dma((px,)), dma((py,)), dma((py,)),
    ] + [dma((2, count, pm)) for _ in range(8)]
    cfg = (nx, ny, ns, rows, width, chunks, early)
    hbm = pl.BlockSpec(memory_space=pltpu.MemorySpace.HBM)
    vm = pl.BlockSpec(memory_space=pltpu.MemorySpace.VMEM)
    out = pl.pallas_call(
        functools.partial(kernel, cfg),
        out_shape=OUT(rows, da, df),
        in_specs=[hbm] * 4,
        out_specs=[vm] * 2,
        scratch_shapes=scratch,
        compiler_params=pltpu.CompilerParams(
            collective_id=0, has_side_effects=True, vmem_limit_bytes=52 * 2**20),
    )(anchor_attn, anchor_ffn, local_attn, local_ffn)
    return write_out(*out)


def write_kernel(a, b, oa, ob, sem):
    pieces = sem.shape[1]
    block = a.shape[0] // pieces
    copies = []
    for k in range(pieces):
        at = pl.ds(k * block, block)
        for q, (src, dst) in enumerate(((b, ob), (a, oa))):
            copy = pltpu.make_async_copy(src.at[at], dst.at[at], sem.at[q, k])
            copy.start()
            copies.append(copy)
    for copy in copies:
        copy.wait()


def write_out(a, b):
    pieces = math.gcd(a.shape[0] // SUB, 4)
    return pl.pallas_call(
        write_kernel,
        out_shape=[jax.ShapeDtypeStruct(v.shape, v.dtype) for v in (a, b)],
        in_specs=[pl.BlockSpec(memory_space=pltpu.MemorySpace.VMEM)] * 2,
        out_specs=[pl.BlockSpec(memory_space=pltpu.MemorySpace.HBM)] * 2,
        scratch_shapes=[pltpu.SemaphoreType.DMA((2, pieces))],
        compiler_params=pltpu.CompilerParams(vmem_limit_bytes=16 * 2**20),
    )(a, b)


def OUT(rows, da, df):
    return [pltpu.VMEM((rows, da), jnp.float32), pltpu.VMEM((rows, df), jnp.float32)]


def solution(mesh):
    n = mesh.shape["rep"]
    nx = max(d for d in range(1, math.isqrt(n) + 1) if n % d == 0)
    placed = (P("shard", None), P("shard", None), P("rep", "shard", None), P("rep", "shard", None))
    return jax.shard_map(
        functools.partial(shards, nx, n // nx, mesh.shape["shard"]),
        mesh=mesh,
        in_specs=placed,
        out_specs=(P("shard", None), P("shard", None)),
        check_vma=False,
    )
```

```python
import functools
import math

import jax
import jax.numpy as jnp
from jax import lax
from jax.experimental import pallas as pl
from jax.experimental.pallas import tpu as pltpu
from jax.sharding import PartitionSpec as P

MESH = pl.DeviceIdType.MESH
LANES = 128
SUB = 8


def kernel(cfg, aa, af, la, lf, oa, of, anc_a, anc_f, loc_a, loc_f,
           recv1_0, recv1_1, sum1_0, sum1_1, recv2_0, recv2_1,
           part_own, part_up, part_down, part_in, fac_own, fac_x, fac_y,
           load_sem, ps, pr, fxs, fxr, fys, fyr,
           s1s, s1r, s2s, s2r, s3s, s3r, s4s, s4r):
    nx, ny, ns, rows, width, chunks, early = cfg
    n = nx * ny
    me_r = lax.axis_index("rep")
    me_s = lax.axis_index("shard")
    x = lax.rem(me_r, nx)
    y = lax.div(me_r, nx)
    loc, anc, out = (loc_a, loc_f), (anc_a, anc_f), (oa, of)
    src = (la, lf)

    def x_peer(i):
        return {"rep": y * nx + i, "shard": me_s}

    def y_peer(i):
        return {"rep": i * nx + x, "shard": me_s}

    def s_peer(i):
        return {"rep": me_r, "shard": i}

    part_in[...] = jnp.zeros_like(part_in)

    has_next, has_prev = me_s < ns - 1, me_s > 0
    barrier = pltpu.get_barrier_semaphore()

    @pl.when(has_next)
    def _():
        pl.semaphore_signal(barrier, inc=1, device_id=s_peer(me_s + 1), device_id_type=MESH)

    @pl.when(has_prev)
    def _():
        pl.semaphore_signal(barrier, inc=1, device_id=s_peer(me_s - 1), device_id_type=MESH)

    for d in range(1, nx):
        pl.semaphore_signal(barrier, inc=1, device_id=x_peer(lax.rem(x + d, nx)), device_id_type=MESH)
    for d in range(1, ny):
        pl.semaphore_signal(barrier, inc=1, device_id=y_peer(lax.rem(y + d, ny)), device_id_type=MESH)
    near = jnp.where(has_next, 1, 0) + jnp.where(has_prev, 1, 0)
    pl.semaphore_wait(barrier, (nx - 1) + (ny - 1) + near)

    paths = (
        (nx, x, x_peer, ny, y, y_peer, recv1_0, sum1_0, recv2_0, fac_x),
        (ny, y, y_peer, nx, x, x_peer, recv1_1, sum1_1, recv2_1, fac_y),
    )
    piece = rows // n

    def remote(a, b, ss, rs, peer):
        return pltpu.make_async_remote_copy(
            src_ref=a, dst_ref=b, send_sem=ss, recv_sem=rs, device_id=peer, device_id_type=MESH)

    def columns(p, c):
        q, col = chunks[p][c]
        return q, pl.ds(col, width), pl.ds(c * width, width)

    count = len(chunks[0])
    stage1, stage2, stage3, stage4 = {}, {}, {}, {}

    def start1(c):
        for p in range(2):
            n1, i1, peer1, n2, i2, peer2, recv1, sum1, recv2, fac = paths[p]
            q, cols, wide = columns(p, c)
            for d in range(1, n1):
                j = lax.rem(i1 + d, n1)
                at = pl.ds(pl.multiple_of(j * (rows // n1), rows // n1), rows // n1)
                copy = remote(src[q].at[0, at, cols], recv1.at[d - 1, :, wide],
                              s1s.at[p, c, d - 1], s1r.at[p, c, d - 1], peer1(j))
                copy.start()
                stage1[p, c, d] = copy

    start1(0)

    pieces = load_sem.shape[1]
    block = rows // pieces
    loads = []
    for k in range(pieces):
        at = pl.ds(k * block, block)
        for q, (a, b) in enumerate(((la.at[0], loc_a), (lf.at[0], loc_f), (aa, anc_a), (af, anc_f))):
            copy = pltpu.make_async_copy(a.at[at], b.at[at], load_sem.at[q, k])
            copy.start()
            loads.append(copy)

    for c in range(1, early):
        start1(c)

    accs = tuple(jnp.zeros((SUB, LANES), jnp.float32) for _ in range(4))
    for k in range(pieces):
        for copy in loads[4 * k:4 * k + 4]:
            copy.wait()

        def body(g, accs):
            accs = list(accs)
            at = pl.ds(pl.multiple_of(k * block + g * SUB, SUB), SUB)
            i = 0
            for q in range(2):
                for t in range(loc[q].shape[1] // LANES):
                    lanes = pl.ds(t * LANES, LANES)
                    delta = loc[q][at, lanes] - anc[q][at, lanes]
                    accs[i % 4] = accs[i % 4] + delta * delta
                    i += 1
            return tuple(accs)

        accs = lax.fori_loop(0, block // SUB, body, accs)
    part_own[...] = (accs[0] + accs[1]) + (accs[2] + accs[3])
    up = remote(part_up, part_in.at[0], ps.at[0], pr.at[0], s_peer(lax.rem(me_s + 1, ns)))
    down = remote(part_down, part_in.at[1], ps.at[1], pr.at[1], s_peer(lax.rem(me_s + ns - 1, ns)))

    def pass_up():
        @pl.when(has_prev)
        def _():
            up.wait_recv()

        part_up[...] = part_own[...] + part_in[0]

        @pl.when(has_next)
        def _():
            up.start()

    def pass_down():
        @pl.when(has_next)
        def _():
            down.wait_recv()

        part_down[...] = part_own[...] + part_in[1]

        @pl.when(has_prev)
        def _():
            down.start()

    @pl.when(me_s < ns // 2)
    def _():
        pass_up()
        pass_down()

    @pl.when(me_s >= ns // 2)
    def _():
        pass_down()
        pass_up()

    total = part_own[...] + (part_in[0] + part_in[1])
    squares = jnp.full((SUB, LANES), jnp.sum(total), jnp.float32)
    fac_own[...] = jnp.minimum(jnp.float32(1.0), 1.0 / jnp.sqrt(squares))
    fx, fy = [], []
    for d in range(1, nx):
        copy = remote(fac_own, fac_x.at[d - 1], fxs.at[d - 1], fxr.at[d - 1], x_peer(lax.rem(x + d, nx)))
        copy.start()
        fx.append(copy)
    for d in range(1, ny):
        copy = remote(fac_own, fac_y.at[d - 1], fys.at[d - 1], fyr.at[d - 1], y_peer(lax.rem(y + d, ny)))
        copy.start()
        fy.append(copy)
    for c in range(early, count):
        start1(c)
    for copy in fx + fy:
        copy.wait_recv()

    for c in range(count):
        for p in range(2):
            n1, i1, peer1, n2, i2, peer2, recv1, sum1, recv2, fac = paths[p]
            q, cols, wide = columns(p, c)
            for d in range(1, n1):
                stage1[p, c, d].wait_recv()
            base = i1 * (rows // n1)
            mine = fac_own[...]
            theirs = [fac[d - 1] for d in range(1, n1)]

            def body(g, carry):
                at = pl.ds(pl.multiple_of(base + g * SUB, SUB), SUB)
                to = pl.ds(pl.multiple_of(g * SUB, SUB), SUB)
                col, off = chunks[p][c][1], c * width
                for t in range(width // LANES):
                    here = pl.ds(col + t * LANES, LANES)
                    there = pl.ds(off + t * LANES, LANES)
                    anchor = anc[q][at, here]
                    value = mine * (loc[q][at, here] - anchor)
                    for d in range(1, n1):
                        value = value + theirs[d - 1] * (recv1[d - 1, to, there] - anchor)
                    sum1[to, there] = value
                return carry

            lax.fori_loop(0, rows // n1 // SUB, body, 0)
            for d in range(1, n2):
                j = lax.rem(i2 + d, n2)
                at = pl.ds(pl.multiple_of(j * piece, piece), piece)
                copy = remote(sum1.at[at, wide], recv2.at[d - 1, :, wide],
                              s2s.at[p, c, d - 1], s2r.at[p, c, d - 1], peer2(j))
                copy.start()
                stage2[p, c, d] = copy

    for c in range(count):
        for p in range(2):
            n1, i1, peer1, n2, i2, peer2, recv1, sum1, recv2, fac = paths[p]
            q, cols, wide = columns(p, c)
            for d in range(1, n2):
                stage2[p, c, d].wait_recv()
            own = i2 * piece
            place = i1 * (rows // n1) + own

            def body(g, carry):
                at = pl.ds(pl.multiple_of(own + g * SUB, SUB), SUB)
                to = pl.ds(pl.multiple_of(g * SUB, SUB), SUB)
                dst = pl.ds(pl.multiple_of(place + g * SUB, SUB), SUB)
                col, off = chunks[p][c][1], c * width
                for t in range(width // LANES):
                    there = pl.ds(off + t * LANES, LANES)
                    value = sum1[at, there]
                    for d in range(1, n2):
                        value = value + recv2[d - 1, to, there]
                    out[q][dst, pl.ds(col + t * LANES, LANES)] = value / n
                return carry

            lax.fori_loop(0, piece // SUB, body, 0)
            at = pl.ds(pl.multiple_of(place, piece), piece)
            for d in range(1, n2):
                copy = remote(out[q].at[at, cols], out[q].at[at, cols],
                              s3s.at[p, c, d - 1], s3r.at[p, c, d - 1], peer2(lax.rem(i2 + d, n2)))
                copy.start()
                stage3[p, c, d] = copy

    for c in range(count):
        for p in range(2):
            n1, i1, peer1, n2, i2, peer2, recv1, sum1, recv2, fac = paths[p]
            q, cols, wide = columns(p, c)
            for d in range(1, n2):
                stage3[p, c, d].wait_recv()
            at = pl.ds(pl.multiple_of(i1 * (rows // n1), rows // n1), rows // n1)
            for d in range(1, n1):
                copy = remote(out[q].at[at, cols], out[q].at[at, cols],
                              s4s.at[p, c, d - 1], s4r.at[p, c, d - 1], peer1(lax.rem(i1 + d, n1)))
                copy.start()
                stage4[p, c, d] = copy

    @pl.when(has_next)
    def _():
        up.wait_send()

    @pl.when(has_prev)
    def _():
        down.wait_send()

    for copy in fx + fy:
        copy.wait_send()
    for stage in (stage1, stage2, stage3):
        for copy in stage.values():
            copy.wait_send()
    for copy in stage4.values():
        copy.wait()


def shards(nx, ny, ns, anchor_attn, anchor_ffn, local_attn, local_ffn):
    rows, da = anchor_attn.shape
    df = anchor_ffn.shape[1]
    width = math.gcd(da // 2, df // 2)
    width = width // 2 if width % (2 * LANES) == 0 else width
    wide = (da + df) // 2
    chunks = tuple(
        tuple([(1, p * (df // 2) + c) for c in range(0, df // 2, width)]
              + [(0, p * (da // 2) + c) for c in range(0, da // 2, width)])
        for p in range(2))
    count = len(chunks[0])
    early = min(8, count)
    pieces = math.gcd(rows // SUB, 4)
    f32 = jnp.float32
    n = nx * ny
    vmem, dma = pltpu.VMEM, pltpu.SemaphoreType.DMA
    px, py = max(nx - 1, 1), max(ny - 1, 1)
    pm = max(px, py)
    scratch = [
        vmem((rows, da), f32), vmem((rows, df), f32), vmem((rows, da), f32), vmem((rows, df), f32),
        vmem((px, rows // nx, wide), f32), vmem((py, rows // ny, wide), f32),
        vmem((rows // nx, wide), f32), vmem((rows // ny, wide), f32),
        vmem((py, rows // n, wide), f32), vmem((px, rows // n, wide), f32),
        vmem((SUB, LANES), f32), vmem((SUB, LANES), f32), vmem((SUB, LANES), f32), vmem((2, SUB, LANES), f32),
        vmem((SUB, LANES), f32), vmem((px, SUB, LANES), f32), vmem((py, SUB, LANES), f32),
        dma((4, pieces)), dma((2,)), dma((2,)),
        dma((px,)), dma((px,)), dma((py,)), dma((py,)),
    ] + [dma((2, count, pm)) for _ in range(8)]
    cfg = (nx, ny, ns, rows, width, chunks, early)
    hbm = pl.BlockSpec(memory_space=pltpu.MemorySpace.HBM)
    vm = pl.BlockSpec(memory_space=pltpu.MemorySpace.VMEM)
    out = pl.pallas_call(
        functools.partial(kernel, cfg),
        out_shape=OUT(rows, da, df),
        in_specs=[hbm] * 4,
        out_specs=[vm] * 2,
        scratch_shapes=scratch,
        compiler_params=pltpu.CompilerParams(
            collective_id=0, has_side_effects=True, vmem_limit_bytes=52 * 2**20),
    )(anchor_attn, anchor_ffn, local_attn, local_ffn)
    return write_out(*out)


def write_kernel(a, b, oa, ob, sem):
    pieces = sem.shape[1]
    block = a.shape[0] // pieces
    copies = []
    for k in range(pieces):
        at = pl.ds(k * block, block)
        for q, (src, dst) in enumerate(((b, ob), (a, oa))):
            copy = pltpu.make_async_copy(src.at[at], dst.at[at], sem.at[q, k])
            copy.start()
            copies.append(copy)
    for copy in copies:
        copy.wait()


def write_out(a, b):
    pieces = math.gcd(a.shape[0] // SUB, 4)
    return pl.pallas_call(
        write_kernel,
        out_shape=[jax.ShapeDtypeStruct(v.shape, v.dtype) for v in (a, b)],
        in_specs=[pl.BlockSpec(memory_space=pltpu.MemorySpace.VMEM)] * 2,
        out_specs=[pl.BlockSpec(memory_space=pltpu.MemorySpace.HBM)] * 2,
        scratch_shapes=[pltpu.SemaphoreType.DMA((2, pieces))],
        compiler_params=pltpu.CompilerParams(vmem_limit_bytes=16 * 2**20),
    )(a, b)


def OUT(rows, da, df):
    return [pltpu.VMEM((rows, da), jnp.float32), pltpu.VMEM((rows, df), jnp.float32)]


def solution(mesh):
    n = mesh.shape["rep"]
    nx = max(d for d in range(1, math.isqrt(n) + 1) if n % d == 0)
    placed = (P("shard", None), P("shard", None), P("rep", "shard", None), P("rep", "shard", None))
    return jax.shard_map(
        functools.partial(shards, nx, n // nx, mesh.shape["shard"]),
        mesh=mesh,
        in_specs=placed,
        out_specs=(P("shard", None), P("shard", None)),
        check_vma=False,
    )
```
